32 devices in a mesh: groups: 2 (over x), turn: 16 (over z, y, core).
Axes of the slice: x: 2, y: 2, z: 4, core: 2. Of those that a mesh axis runs over, the one named last changes fastest.
Arguments:
- raw_pulses: bfloat16 [2, 4096, 16384], P(None, ('groups', 'turn')), parts along dimension 1, may hold values from -6 to 6
- chirp_taps: bfloat16 [2, 4096], replicated, may hold values from -0.0625 to 0.0625
- knot_points: float32 [256], P(('groups', 'turn')), parts along dimension 0, may hold values from -5 to 5
- knot_index: int32 [4096], P(('groups', 'turn')), parts along dimension 0, may hold values from 0 to 127, as said below
- spline_param: float32 [4096], P(('groups', 'turn')), parts along dimension 0, may hold values from 0 to 1
- migration: int32 [128], P(('groups', 'turn')), parts along dimension 0, may hold values from 0 to 511
- azimuth_rate: float32 [1024], P(('groups', 'turn')), parts along dimension 0, may hold values from 0.02 to 0.5
Outputs:
- focused_image: float32 [2, 1024, 2048], P(None, ('groups', 'turn')), parts along dimension 1
The draws below stay inside these ranges and needn't reach their ends.
There are 2 independent parts, one for each index of `groups`. The reference program is written for one: setup_inputs(seed, part) draws one part's arguments, and reference() takes and returns one part's arrays. A program takes and returns all parts, laid end to end along the dimension named above; an argument that names none is the same for every part. Nothing has to cross between parts.
Inputs may be any that keep to these rules, and one draw needn't show every extreme that they name: `knot_index`: Nondecreasing; the pulses p with p // 128 = d use knots d * 8 to d * 8 + 7, the first such pulse the lowest and the last such pulse the highest of them.
All inputs are finite; a program needn't handle non-finite values.
Results may differ from the reference program's by a relative error of at most 0.011.
Values may be sent and summed in bfloat16 or wider, within the bound.
A program may use at most 64 MiB of HBM per device.

```python
import math
import jax
import jax.numpy as jnp
from jax import lax

R_OUTER = 128
R_INNER = 128
TAPS = 4096
PUL_DEV = 128
BIN_DEV = 32
BLK = 32
MIGMAX = 512
KNOT_DEV = 8
RANGE = 16384
PULSES = 2048
BINS = 512
NBLOCKS = 64
KNOTS = 128
N_TURN = 16


def draw_knot_index(key, part):
    devices_count = PULSES // PUL_DEV
    local = jax.random.randint(key, (devices_count, PUL_DEV), 0, KNOT_DEV)
    local = jnp.sort(local, axis=1)
    local = local.at[:, 0].set(0).at[:, PUL_DEV - 1].set(KNOT_DEV - 1)
    base = jnp.arange(devices_count, dtype=jnp.int32)[:, None] * KNOT_DEV
    return (local + base).reshape(devices_count * PUL_DEV).astype(jnp.int32)


def draw_migration(key, part):
    first_key, second_key = jax.random.split(key)
    values = jax.random.randint(first_key, (NBLOCKS,), 0, MIGMAX)
    spot = jax.random.randint(second_key, (), 0, NBLOCKS)
    values = values.at[spot].set(MIGMAX - 1)
    values = values.at[(spot + NBLOCKS // 2) % NBLOCKS].set(0)
    return values.astype(jnp.int32)


def level_of(key, shape, cuts, smallest, high):
    def one(dim, parts):
        heights = jax.random.uniform(jax.random.fold_in(jax.random.fold_in(key, 6), dim), (parts,), jnp.float32, smallest / len(cuts), high / len(cuts))
        return jnp.repeat(jnp.exp(heights), shape[dim] // parts).reshape((-1,) + (1,) * (len(shape) - dim - 1))

    factor_of = one(*cuts[0])
    for cut in cuts[1:]:
        factor_of = factor_of * one(*cut)
    return factor_of


def noise(key, dims, width, limit, pieces=(), kind=jnp.bfloat16):
    gain = level_of(key, dims, pieces, -0.22, 0.18) if pieces else 1.0
    entries = jax.random.normal(key, dims, jnp.float32) * width * gain
    return jnp.minimum(jnp.maximum(entries, -limit), limit).astype(kind)


def setup_inputs(seed: int = 0, part: int = 0) -> dict:
    key_list = jax.random.split(jax.random.key(seed), 8)
    own_keys = jax.random.split(jax.random.fold_in(key_list[7], part), 8)
    raw_pulses = noise(own_keys[0], (2, PULSES, RANGE), 1.0, 6.0, ((1, 16),))
    chirp_taps = noise(key_list[1], (2, TAPS), (2 * TAPS) ** -0.5, 0.0625)
    knot_points = noise(own_keys[2], (KNOTS,), 1.0, 5.0, ((0, 16),), jnp.float32)
    knot_index = draw_knot_index(jax.random.fold_in(jax.random.fold_in(key_list[7], part), 71), part)
    spline_param = jnp.clip(1.0 * jax.random.uniform(own_keys[4], (PULSES,), jnp.float32) ** level_of(own_keys[4], (PULSES,), ((0, 16),), -0.2, 0.2), 0.0, 1.0)
    migration = draw_migration(jax.random.fold_in(jax.random.fold_in(key_list[7], part), 71), part)
    azimuth_rate = jnp.clip(jnp.exp(math.log(0.5) - 3.218876 * jax.random.uniform(own_keys[6], (BINS,), jnp.float32) ** level_of(own_keys[6], (BINS,), ((0, 16),), -0.2, 0.2)), 0.02, 0.5)
    return {"raw_pulses": raw_pulses, "chirp_taps": chirp_taps, "knot_points": knot_points, "knot_index": knot_index, "spline_param": spline_param, "migration": migration, "azimuth_rate": azimuth_rate}


def dft_table(length, sign):
    line = jnp.arange(length, dtype=jnp.int32)
    product = (line[:, None] * line[None, :]) % length
    angles = product.astype(jnp.float32) * (2.0 * math.pi / length)
    cosine = jnp.cos(angles)
    sine_part = jnp.sin(angles) * sign
    upper = jnp.stack([cosine, -sine_part])
    lower = jnp.stack([sine_part, cosine])
    return jnp.stack([upper, lower]).astype(jnp.bfloat16)


def twiddle(outer, inner, sign):
    outer_line = jnp.arange(outer, dtype=jnp.int32)[:, None]
    inner_line = jnp.arange(inner, dtype=jnp.int32)[None, :]
    product = (outer_line * inner_line) % (outer * inner)
    angles = product.astype(jnp.float32) * (2.0 * math.pi / (outer * inner))
    return jnp.cos(angles), jnp.sin(angles) * sign


def rotate_by(signal, real_part, imag_part):
    return jnp.stack([signal[0] * real_part - signal[1] * imag_part,
                      signal[0] * imag_part + signal[1] * real_part])


def along_outer(matrix, signal):
    return jnp.einsum("dcak,cbaj->dbkj", matrix.astype(jnp.float32), signal.astype(jnp.float32),
                      precision=lax.Precision.HIGHEST)


def along_inner(matrix, signal):
    return jnp.einsum("dcak,cbia->dbik", matrix.astype(jnp.float32), signal.astype(jnp.float32),
                      precision=lax.Precision.HIGHEST)


def forward(signal, outer, inner):
    section = along_outer(dft_table(outer, -1.0), signal)
    real_part, imag_part = twiddle(outer, inner, -1.0)
    section = rotate_by(section, real_part, imag_part).astype(jnp.bfloat16)
    return along_inner(dft_table(inner, -1.0), section)


def backward(spectrum, outer, inner):
    section = along_inner(dft_table(inner, 1.0), spectrum)
    real_part, imag_part = twiddle(outer, inner, 1.0)
    section = rotate_by(section, real_part, imag_part).astype(jnp.bfloat16)
    return along_outer(dft_table(outer, 1.0), section)


def spline_weights(position):
    rest = 1.0 - position
    square = position * position
    cube = square * position
    return (rest * rest * rest / 6.0,
            (3.0 * cube - 6.0 * square + 4.0) / 6.0,
            (-3.0 * cube + 3.0 * square + 3.0 * position + 1.0) / 6.0,
            cube / 6.0)


def frequency_square(outer, inner):
    total = outer * inner
    freq = jnp.arange(outer, dtype=jnp.int32)[:, None] + outer * jnp.arange(inner, dtype=jnp.int32)[None, :]
    centred = jnp.where(freq < total // 2, freq, freq - total)
    return (centred * centred).astype(jnp.float32) / total


def reference(raw_pulses, chirp_taps, knot_points, knot_index, spline_param, migration, azimuth_rate):
    padded = jnp.pad(chirp_taps, ((0, 0), (0, RANGE - TAPS))).reshape(2, 1, R_OUTER, R_INNER)
    chirp_spec = forward(padded, R_OUTER, R_INNER)[:, 0]
    extended = jnp.concatenate([knot_points, jnp.zeros((3,), jnp.float32)])
    weights = spline_weights(spline_param)
    displace = weights[0] * extended[knot_index]
    for step in range(1, 4):
        displace = displace + weights[step] * extended[knot_index + step]
    phase = -4.0 * math.pi * displace
    cos_all = jnp.cos(phase)
    sin_all = jnp.sin(phase)

    def compress(block_id):
        start = (block_id * BLK).astype(jnp.int32)
        pulse_block = lax.dynamic_slice_in_dim(raw_pulses, start, BLK, 1).reshape(2, BLK, R_OUTER, R_INNER)
        spectrum = forward(pulse_block, R_OUTER, R_INNER)
        matched = rotate_by(spectrum, chirp_spec[0][None], -chirp_spec[1][None]).astype(jnp.bfloat16)
        full = backward(matched, R_OUTER, R_INNER).reshape(2, BLK, RANGE) * (1.0 / RANGE)
        offset = migration[block_id].astype(jnp.int32)
        window = lax.dynamic_slice_in_dim(full, offset, BINS, 2)
        cos_block = lax.dynamic_slice_in_dim(cos_all, start, BLK, 0)
        sin_block = lax.dynamic_slice_in_dim(sin_all, start, BLK, 0)
        return rotate_by(window, cos_block[:, None], sin_block[:, None]).astype(jnp.bfloat16)

    stacked = lax.map(compress, jnp.arange(NBLOCKS, dtype=jnp.int32))
    columns = jnp.transpose(stacked, (1, 3, 0, 2)).reshape(2, N_TURN, BIN_DEV, PULSES)
    grouped = jnp.transpose(columns, (1, 0, 2, 3))
    rates = azimuth_rate.reshape(N_TURN, BIN_DEV)
    quad = frequency_square(N_TURN, PUL_DEV)

    def focus(item):
        group, rate = item
        spectrum = forward(group.reshape(2, BIN_DEV, N_TURN, PUL_DEV), N_TURN, PUL_DEV)
        angle_map = math.pi * rate[:, None, None] * quad[None]
        focused = rotate_by(spectrum, jnp.cos(angle_map), jnp.sin(angle_map)).astype(jnp.bfloat16)
        return backward(focused, N_TURN, PUL_DEV).reshape(2, BIN_DEV, PULSES) * (1.0 / PULSES)

    images = lax.map(focus, (grouped, rates))
    return jnp.transpose(images, (1, 0, 2, 3)).reshape(2, BINS, PULSES)
```

```python
import functools
import math

import jax
import jax.numpy as jnp
import numpy as np
from jax import lax
from jax.experimental import pallas as pl
from jax.experimental.pallas import tpu as pltpu
from jax.sharding import PartitionSpec as P

BLK = 32
MIGMAX = 512
LANES = 128
F32 = jnp.float32
BF16 = jnp.bfloat16


def table_np(length, sign):
    line = np.arange(length)
    angles = (line[:, None] * line[None, :] % length) * (2.0 * math.pi / length)
    c, s = np.cos(angles), np.sin(angles) * sign
    return np.concatenate(
        [np.concatenate([c, s], 1), np.concatenate([-s, c], 1)], 0
    ).astype(BF16)


def twiddle_np(outer, inner, sign, scale):
    angles = (np.arange(outer)[:, None] * np.arange(inner)[None, :] % (outer * inner)) * (
        2.0 * math.pi / (outer * inner)
    )
    return np.stack([np.cos(angles) * scale, np.sin(angles) * sign * scale]).astype(np.float32)


def transform(values, sign):
    n = len(values)
    if n == 1:
        return values
    even = transform(values[0::2], sign)
    odd = transform(values[1::2], sign)
    low, high = [], []
    for k in range(n // 2):
        (er, ei), (zr, zi) = even[k], odd[k]
        if k == 0:
            tr, ti = zr, zi
        elif 4 * k == n:
            tr, ti = (-zi, zr) if sign > 0 else (zi, -zr)
        elif 8 * k == n:
            h = math.sqrt(0.5)
            tr, ti = ((zr - zi) * h, (zr + zi) * h) if sign > 0 else ((zr + zi) * h, (zi - zr) * h)
        elif 8 * k == 3 * n:
            h = math.sqrt(0.5)
            tr, ti = (
                ((-zr - zi) * h, (zr - zi) * h) if sign > 0 else ((zi - zr) * h, (-zr - zi) * h)
            )
        else:
            c = math.cos(2 * math.pi * k / n)
            s = math.sin(2 * math.pi * k / n) * sign
            tr, ti = zr * c - zi * s, zr * s + zi * c
        low.append((er + tr, ei + ti))
        high.append((er - tr, ei - ti))
    return low + high


def cos_sin_quarters(quarters):
    whole = jnp.floor(quarters + 0.5)
    x = (quarters - whole) * (0.5 * math.pi)
    n = whole.astype(jnp.int32)
    z = x * x
    s = x + x * z * ((-1.9515295891e-4 * z + 8.3321608736e-3) * z - 1.6666654611e-1)
    c = 1.0 - 0.5 * z + z * z * (
        (2.443315711809948e-5 * z - 1.388731625493765e-3) * z + 4.166664568298827e-2
    )
    odd = (n & 1) == 1
    cos = jnp.where(odd, s, c)
    sin = jnp.where(odd, c, s)
    cos = jnp.where(((n + 1) & 2) == 2, -cos, cos)
    sin = jnp.where((n & 2) == 2, -sin, sin)
    return cos, sin


def build_taps(chirp_ref, taps_ref, columns):
    sub = lax.broadcasted_iota(jnp.int32, (LANES, LANES), 0)
    lane = lax.broadcasted_iota(jnp.int32, (LANES, LANES), 1)
    keep = lane >= sub
    for d in range(2):
        before = jnp.zeros((LANES, LANES), F32)
        for block in range(columns + 1):
            if block < columns:
                row = chirp_ref[d : d + 1, block * LANES : (block + 1) * LANES].astype(F32)
                turned = pltpu.roll(
                    jnp.broadcast_to(row, (LANES, LANES)), 0, 1, stride=1, stride_axis=0
                )
            else:
                turned = jnp.zeros((LANES, LANES), F32)
            taps_ref[d * LANES : (d + 1) * LANES, block * LANES : (block + 1) * LANES] = jnp.where(
                keep, turned, before
            ).astype(BF16)
            before = turned


def shift_block(raw_ref, moved_ref, offset, block, columns):
    whole = offset // LANES
    part = offset - whole * LANES
    lane = lax.broadcasted_iota(jnp.int32, (BLK, LANES), 1)
    keep = lane < LANES - part
    turn_by = lax.rem(LANES - part, LANES)
    rows = slice(block * BLK, (block + 1) * BLK)
    for c in range(2):
        before = None
        for j in range(columns + 1):
            start = pl.multiple_of(whole * LANES + j * LANES, LANES)
            piece = raw_ref[c, rows, pl.ds(start, LANES)].astype(F32)
            piece = pltpu.roll(piece, turn_by, 1)
            if before is not None:
                moved_ref[c, rows, (j - 1) * LANES : j * LANES] = jnp.where(
                    keep, before, piece
                ).astype(BF16)
            before = piece


def phases(knot_at, slots, knot_local, position):
    rest = 1.0 - position
    square = position * position
    cube = square * position
    weights = (
        rest * rest * rest / 6.0,
        (3.0 * cube - 6.0 * square + 4.0) / 6.0,
        (-3.0 * cube + 3.0 * square + 3.0 * position + 1.0) / 6.0,
        cube / 6.0,
    )
    displace = jnp.zeros_like(position)
    for step in range(4):
        value = jnp.zeros_like(position)
        for slot in range(slots):
            value = jnp.where(knot_local + step == slot, knot_at(slot), value)
        displace = displace + weights[step] * value
    return cos_sin_quarters(-8.0 * displace)


def compress_bins(taps_ref, moved_ref, start, width, cos, sin):
    samples = jnp.concatenate(
        [moved_ref[0, :, pl.ds(start, width)], moved_ref[1, :, pl.ds(start, width)]], axis=0
    )
    both = lax.dot_general(
        taps_ref[...], samples, (((1,), (1,)), ((), ())), preferred_element_type=F32
    )
    half = both.shape[1] // 2
    real = both[:LANES, :half] + both[LANES:, half:]
    imag = both[:LANES, half:] - both[LANES:, :half]
    return (real * cos - imag * sin).astype(BF16), (real * sin + imag * cos).astype(BF16)


def focus_maps(rate_at, bins, turn_count, inner, cos_ref, sin_ref):
    sub = lax.broadcasted_iota(jnp.int32, (bins, inner), 0)
    rate = jnp.zeros((bins, inner), F32)
    for r in range(bins):
        rate = jnp.where(sub == r, rate_at(r), rate)
    total = turn_count * inner
    lane = lax.broadcasted_iota(jnp.int32, (1, inner), 1)

    def one(k2):
        freq = k2 + turn_count * lane
        centred = jnp.where(freq < total // 2, freq, freq - total)
        quad = (centred * centred).astype(F32) * (2.0 / total)
        cos, sin = cos_sin_quarters(rate * quad)
        at = k2 * bins
        if not isinstance(k2, int):
            at = pl.multiple_of(at, bins)
        cos_ref[pl.ds(at, bins), :] = cos
        sin_ref[pl.ds(at, bins), :] = sin

    if turn_count <= 16:
        for k2 in range(turn_count):
            one(k2)
    else:
        pl.loop(0, turn_count)(one)


def azimuth(inbox_ref, gm_ref, gp_ref, fm_ref, fp_ref, cos_ref, sin_ref, half_ref, spec_ref, out_ref):
    turn_count, _, bins, inner = inbox_ref.shape
    step = 16
    rows = turn_count * bins
    chunk = min(rows, 512)
    for r in range(0, bins, step):
        values = [
            (
                inbox_ref[s, 0, r : r + step, :].astype(F32),
                inbox_ref[s, 1, r : r + step, :].astype(F32),
            )
            for s in range(turn_count)
        ]
        for k2, (re, im) in enumerate(transform(values, -1)):
            if k2:
                gr, gi = gm_ref[0, k2 : k2 + 1, :], gm_ref[1, k2 : k2 + 1, :]
                re, im = re * gr - im * gi, re * gi + im * gr
            at = k2 * bins + r
            half_ref[at : at + step, :inner] = re.astype(BF16)
            half_ref[at : at + step, inner:] = im.astype(BF16)
    for at in range(0, rows, chunk):
        here = slice(at, at + chunk)
        spec = jnp.dot(half_ref[here, :], fm_ref[...], preferred_element_type=F32)
        sr, si = spec[:, :inner], spec[:, inner:]
        cr, ci = cos_ref[here, :], sin_ref[here, :]
        half_ref[here, :inner] = (sr * cr - si * ci).astype(BF16)
        half_ref[here, inner:] = (sr * ci + si * cr).astype(BF16)
    for at in range(0, rows, chunk):
        here = slice(at, at + chunk)
        spec_ref[here, :] = jnp.dot(half_ref[here, :], fp_ref[...], preferred_element_type=F32)
    for r in range(0, bins, step):
        values = []
        for k2 in range(turn_count):
            at = k2 * bins + r
            re, im = spec_ref[at : at + step, :inner], spec_ref[at : at + step, inner:]
            gr, gi = gp_ref[0, k2 : k2 + 1, :], gp_ref[1, k2 : k2 + 1, :]
            values.append((re * gr - im * gi, re * gi + im * gr))
        for n2, (re, im) in enumerate(transform(values, 1)):
            out_ref[0, r : r + step, n2 * inner : (n2 + 1) * inner] = re
            out_ref[1, r : r + step, n2 * inner : (n2 + 1) * inner] = im


def range_kernel(migration, knots, raw, chirp, index, position, out, taps, moved, *, columns, bins_total, bin_local):
    slots = knots.shape[0]
    build_taps(chirp, taps, columns)
    for block in range(raw.shape[1] // BLK):
        shift_block(raw, moved, migration[block], block, moved.shape[2] // LANES)
    cos, sin = phases(lambda j: knots[j], slots, index[...], position[...])
    per = LANES // bin_local
    width = (columns + 1) * LANES

    def one(j):
        re, im = compress_bins(taps, moved, pl.multiple_of(j * LANES, LANES), width, cos, sin)
        for u in range(per):
            out[j * per + u, 0] = re[u * bin_local : (u + 1) * bin_local]
            out[j * per + u, 1] = im[u * bin_local : (u + 1) * bin_local]

    pl.loop(0, bins_total // LANES)(one)


def focus_kernel(rate, inbox, gm, gp, fm, fp, out, cos, sin, half, spec):
    turn_count, _, bins, inner = inbox.shape
    focus_maps(lambda r: rate[r], bins, turn_count, inner, cos, sin)
    azimuth(inbox, gm, gp, fm, fp, cos, sin, half, spec, out)


def local(raw_pulses, chirp_taps, knot_points, knot_index, spline_param, migration, azimuth_rate):
    turn_count = lax.axis_size("turn")
    pulses = raw_pulses.shape[1]
    taps_count = chirp_taps.shape[1]
    bin_local = azimuth_rate.shape[0]
    bins_total = bin_local * turn_count
    columns = taps_count // LANES
    width = bins_total + taps_count
    reach = width + MIGMAX
    pairs = [(i, i - 1) for i in range(1, turn_count)]
    next_points = lax.ppermute(knot_points[:3], "turn", pairs)
    knots = jnp.concatenate([knot_points, next_points])
    knot_local = knot_index - lax.axis_index("turn") * knot_points.shape[0]
    smem = pl.BlockSpec(memory_space=pltpu.SMEM)
    vmem = pl.BlockSpec(memory_space=pltpu.VMEM)
    sent = pl.pallas_call(
        functools.partial(range_kernel, columns=columns, bins_total=bins_total, bin_local=bin_local),
        grid=(1,),
        in_specs=[
            smem,
            smem,
            pl.BlockSpec((2, pulses, reach), lambda i: (0, 0, 0)),
            vmem,
            vmem,
            vmem,
        ],
        out_specs=vmem,
        out_shape=jax.ShapeDtypeStruct((turn_count, 2, bin_local, pulses), BF16),
        scratch_shapes=[
            pltpu.VMEM((2 * LANES, taps_count + LANES), BF16),
            pltpu.VMEM((2, pulses, width), BF16),
        ],
        compiler_params=pltpu.CompilerParams(vmem_limit_bytes=60 * 2**20),
    )(migration, knots, raw_pulses, chirp_taps, knot_local.reshape(1, -1), spline_param.reshape(1, -1))
    inbox = lax.all_to_all(sent, "turn", split_axis=0, concat_axis=0, tiled=True)
    gm = twiddle_np(turn_count, pulses, -1.0, 1.0)
    gp = twiddle_np(turn_count, pulses, 1.0, 1.0 / (turn_count * pulses))
    rows = turn_count * bin_local
    return pl.pallas_call(
        focus_kernel,
        in_specs=[smem] + [vmem] * 5,
        out_specs=vmem,
        out_shape=jax.ShapeDtypeStruct((2, bin_local, turn_count * pulses), F32),
        scratch_shapes=[
            pltpu.VMEM((rows, pulses), F32),
            pltpu.VMEM((rows, pulses), F32),
            pltpu.VMEM((rows, 2 * pulses), BF16),
            pltpu.VMEM((rows, 2 * pulses), F32),
        ],
        compiler_params=pltpu.CompilerParams(vmem_limit_bytes=60 * 2**20),
    )(azimuth_rate, inbox, gm, gp, table_np(pulses, -1.0), table_np(pulses, 1.0))


def solution(mesh):
    in_specs = (
        P(None, ("groups", "turn"), None),
        P(),
        P(("groups", "turn")),
        P(("groups", "turn")),
        P(("groups", "turn")),
        P(("groups", "turn")),
        P(("groups", "turn")),
    )
    out_specs = P(None, ("groups", "turn"), None)
    return jax.shard_map(local, mesh=mesh, in_specs=in_specs, out_specs=out_specs, check_vma=False)
```

```python
import functools
import math

import jax
import jax.numpy as jnp
import numpy as np
from jax import lax
from jax.experimental import pallas as pl
from jax.experimental.pallas import tpu as pltpu
from jax.sharding import PartitionSpec as P

BLK = 32
MIGMAX = 512
LANES = 128
F32 = jnp.float32
BF16 = jnp.bfloat16


def table_np(length, sign):
    line = np.arange(length)
    angles = (line[:, None] * line[None, :] % length) * (2.0 * math.pi / length)
    c, s = np.cos(angles), np.sin(angles) * sign
    return np.concatenate(
        [np.concatenate([c, s], 1), np.concatenate([-s, c], 1)], 0
    ).astype(BF16)


def twiddle_np(outer, inner, sign, scale):
    angles = (np.arange(outer)[:, None] * np.arange(inner)[None, :] % (outer * inner)) * (
        2.0 * math.pi / (outer * inner)
    )
    return np.stack([np.cos(angles) * scale, np.sin(angles) * sign * scale]).astype(np.float32)


def transform(values, sign):
    n = len(values)
    if n == 1:
        return values
    even = transform(values[0::2], sign)
    odd = transform(values[1::2], sign)
    low, high = [], []
    for k in range(n // 2):
        (er, ei), (zr, zi) = even[k], odd[k]
        if k == 0:
            tr, ti = zr, zi
        elif 4 * k == n:
            tr, ti = (-zi, zr) if sign > 0 else (zi, -zr)
        elif 8 * k == n:
            h = math.sqrt(0.5)
            tr, ti = ((zr - zi) * h, (zr + zi) * h) if sign > 0 else ((zr + zi) * h, (zi - zr) * h)
        elif 8 * k == 3 * n:
            h = math.sqrt(0.5)
            tr, ti = (
                ((-zr - zi) * h, (zr - zi) * h) if sign > 0 else ((zi - zr) * h, (-zr - zi) * h)
            )
        else:
            c = math.cos(2 * math.pi * k / n)
            s = math.sin(2 * math.pi * k / n) * sign
            tr, ti = zr * c - zi * s, zr * s + zi * c
        low.append((er + tr, ei + ti))
        high.append((er - tr, ei - ti))
    return low + high


def cos_sin_quarters(quarters):
    whole = jnp.floor(quarters + 0.5)
    x = (quarters - whole) * (0.5 * math.pi)
    n = whole.astype(jnp.int32)
    z = x * x
    s = x + x * z * ((-1.9515295891e-4 * z + 8.3321608736e-3) * z - 1.6666654611e-1)
    c = 1.0 - 0.5 * z + z * z * (
        (2.443315711809948e-5 * z - 1.388731625493765e-3) * z + 4.166664568298827e-2
    )
    odd = (n & 1) == 1
    cos = jnp.where(odd, s, c)
    sin = jnp.where(odd, c, s)
    cos = jnp.where(((n + 1) & 2) == 2, -cos, cos)
    sin = jnp.where((n & 2) == 2, -sin, sin)
    return cos, sin


def build_taps(chirp_ref, taps_ref, columns):
    sub = lax.broadcasted_iota(jnp.int32, (LANES, LANES), 0)
    lane = lax.broadcasted_iota(jnp.int32, (LANES, LANES), 1)
    keep = lane >= sub
    for d in range(2):
        before = jnp.zeros((LANES, LANES), F32)
        for block in range(columns + 1):
            if block < columns:
                row = chirp_ref[d : d + 1, block * LANES : (block + 1) * LANES].astype(F32)
                turned = pltpu.roll(
                    jnp.broadcast_to(row, (LANES, LANES)), 0, 1, stride=1, stride_axis=0
                )
            else:
                turned = jnp.zeros((LANES, LANES), F32)
            taps_ref[d * LANES : (d + 1) * LANES, block * LANES : (block + 1) * LANES] = jnp.where(
                keep, turned, before
            ).astype(BF16)
            before = turned


def pick_rows(ref, start, offsets):
    def chosen(x, bit):
        return (jnp.broadcast_to(offsets, x.shape) & bit) != 0

    bit = MIGMAX // 2
    size = LANES + bit
    low = ref[pl.ds(start, size), :]
    x = jnp.where(chosen(low, bit), ref[pl.ds(start + bit, size), :], low)
    while bit > 8:
        bit //= 2
        size = LANES + bit
        low = x[:size]
        x = jnp.where(chosen(low, bit), x[bit : bit + size], low)
    while bit > 1:
        bit //= 2
        x = jnp.where(chosen(x, bit), pltpu.roll(x, x.shape[0] - bit, 0), x)
    return x[:LANES]


def phases(knot_at, slots, knot_local, position):
    rest = 1.0 - position
    square = position * position
    cube = square * position
    weights = (
        rest * rest * rest / 6.0,
        (3.0 * cube - 6.0 * square + 4.0) / 6.0,
        (-3.0 * cube + 3.0 * square + 3.0 * position + 1.0) / 6.0,
        cube / 6.0,
    )
    displace = jnp.zeros_like(position)
    for step in range(4):
        value = jnp.zeros_like(position)
        for slot in range(slots):
            value = jnp.where(knot_local + step == slot, knot_at(slot), value)
        displace = displace + weights[step] * value
    return cos_sin_quarters(-8.0 * displace)


def compress_block(taps_ref, raw_ref, block, width, real_ref, imag_ref):
    here = pl.ds(pl.multiple_of(block * LANES, LANES), width)
    samples = jnp.concatenate([raw_ref[0, :, here], raw_ref[1, :, here]], axis=0)
    both = lax.dot_general(
        taps_ref[...], samples, (((1,), (1,)), ((), ())), preferred_element_type=F32
    )
    half = both.shape[1] // 2
    rows = pl.ds(pl.multiple_of(block * LANES, LANES), LANES)
    real_ref[rows, :] = both[:LANES, :half] + both[LANES:, half:]
    imag_ref[rows, :] = both[:LANES, half:] - both[LANES:, :half]


def focus_maps(rate_at, bins, turn_count, inner, cos_ref, sin_ref):
    sub = lax.broadcasted_iota(jnp.int32, (bins, inner), 0)
    rate = jnp.zeros((bins, inner), F32)
    for r in range(bins):
        rate = jnp.where(sub == r, rate_at(r), rate)
    total = turn_count * inner
    lane = lax.broadcasted_iota(jnp.int32, (1, inner), 1)

    def one(k2):
        freq = k2 + turn_count * lane
        centred = jnp.where(freq < total // 2, freq, freq - total)
        quad = (centred * centred).astype(F32) * (2.0 / total)
        cos, sin = cos_sin_quarters(rate * quad)
        at = k2 * bins
        if not isinstance(k2, int):
            at = pl.multiple_of(at, bins)
        cos_ref[pl.ds(at, bins), :] = cos
        sin_ref[pl.ds(at, bins), :] = sin

    if turn_count <= 16:
        for k2 in range(turn_count):
            one(k2)
    else:
        pl.loop(0, turn_count)(one)


def azimuth(inbox_ref, gm_ref, gp_ref, fm_ref, fp_ref, cos_ref, sin_ref, half_ref, spec_ref, out_ref):
    turn_count, _, bins, inner = inbox_ref.shape
    step = 16
    rows = turn_count * bins
    chunk = min(rows, 512)
    for r in range(0, bins, step):
        values = [
            (
                inbox_ref[s, 0, r : r + step, :].astype(F32),
                inbox_ref[s, 1, r : r + step, :].astype(F32),
            )
            for s in range(turn_count)
        ]
        for k2, (re, im) in enumerate(transform(values, -1)):
            if k2:
                gr, gi = gm_ref[0, k2 : k2 + 1, :], gm_ref[1, k2 : k2 + 1, :]
                re, im = re * gr - im * gi, re * gi + im * gr
            at = k2 * bins + r
            half_ref[at : at + step, :inner] = re.astype(BF16)
            half_ref[at : at + step, inner:] = im.astype(BF16)
    for at in range(0, rows, chunk):
        here = slice(at, at + chunk)
        spec = jnp.dot(half_ref[here, :], fm_ref[...], preferred_element_type=F32)
        sr, si = spec[:, :inner], spec[:, inner:]
        cr, ci = cos_ref[here, :], sin_ref[here, :]
        half_ref[here, :inner] = (sr * cr - si * ci).astype(BF16)
        half_ref[here, inner:] = (sr * ci + si * cr).astype(BF16)
    for at in range(0, rows, chunk):
        here = slice(at, at + chunk)
        spec_ref[here, :] = jnp.dot(half_ref[here, :], fp_ref[...], preferred_element_type=F32)
    for r in range(0, bins, step):
        values = []
        for k2 in range(turn_count):
            at = k2 * bins + r
            re, im = spec_ref[at : at + step, :inner], spec_ref[at : at + step, inner:]
            gr, gi = gp_ref[0, k2 : k2 + 1, :], gp_ref[1, k2 : k2 + 1, :]
            values.append((re * gr - im * gi, re * gi + im * gr))
        for n2, (re, im) in enumerate(transform(values, 1)):
            out_ref[0, r : r + step, n2 * inner : (n2 + 1) * inner] = re
            out_ref[1, r : r + step, n2 * inner : (n2 + 1) * inner] = im


def kernel(
    migration, knots, rate, chirp, index, position, raw_hbm, gm_hbm, gp_hbm, fm_hbm, fp_hbm,
    out,
    raw, gm, gp, fm, fp, taps, real, imag, own_knots, next_knots, outbox, inbox, cos_map, sin_map, half, spec,
    load_sem, knot_sem, send_sem, recv_sem, self_sem,
):
    turn_count, _, bin_local, pulses = inbox.shape
    knot_count = knots.shape[0]
    per = LANES // bin_local
    blocks = turn_count // per
    columns = chirp.shape[1] // LANES
    me = lax.axis_index("turn")
    mine, lane_of_me = lax.div(me, per), lax.rem(me, per)
    mesh_id = pl.DeviceIdType.MESH
    loads = [
        pltpu.make_async_copy(src, dst, load_sem.at[i])
        for i, (src, dst) in enumerate(
            [
                (raw_hbm.at[:, :, pl.ds(0, raw.shape[2])], raw),
                (gm_hbm, gm),
                (gp_hbm, gp),
                (fm_hbm, fm),
                (fp_hbm, fp),
            ]
        )
    ]
    for load in loads:
        load.start()
    barrier = pltpu.get_barrier_semaphore()

    def greet(off):
        pl.semaphore_signal(
            barrier, inc=1, device_id={"turn": lax.rem(me + off, turn_count)}, device_id_type=mesh_id
        )

    if turn_count <= 16:
        for off in range(1, turn_count):
            greet(off)
    else:
        pl.loop(1, turn_count)(greet)
    for j in range(min(knot_count, 8)):
        own_knots[j : j + 1, :] = jnp.full((1, LANES), knots[j], F32)
    build_taps(chirp, taps, columns)
    pl.semaphore_wait(barrier, turn_count - 1)
    knot_copy = pltpu.make_async_remote_copy(
        src_ref=own_knots,
        dst_ref=next_knots,
        send_sem=knot_sem.at[0],
        recv_sem=knot_sem.at[1],
        device_id={"turn": lax.rem(me + turn_count - 1, turn_count)},
        device_id_type=mesh_id,
    )
    knot_copy.start()
    loads[0].wait()
    width = (columns + 1) * LANES
    extra = MIGMAX // LANES
    upward = mine >= blocks // 2

    def compress(i):
        block = jnp.where(upward, i, blocks + extra - 1 - i)
        compress_block(taps, raw, block, width, real, imag)

    for i in range(extra):
        compress(i)
    knot_copy.wait()
    past = jnp.where(me == turn_count - 1, 0.0, 1.0).astype(F32)

    def knot_at(slot):
        if slot < knot_count:
            return knots[slot]
        return next_knots[slot - knot_count : slot - knot_count + 1, :] * past

    cos, sin = phases(knot_at, knot_count + 3, index[...] - me * knot_count, position[...])
    pulse = lax.broadcasted_iota(jnp.int32, (1, pulses), 1)
    offsets = jnp.zeros((1, pulses), jnp.int32)
    for block in range(pulses // BLK):
        offsets = jnp.where(pulse // BLK == block, migration[block], offsets)

    def message(peer, sender):
        return pltpu.make_async_remote_copy(
            src_ref=outbox.at[peer],
            dst_ref=inbox.at[sender],
            send_sem=send_sem.at[peer],
            recv_sem=recv_sem.at[sender],
            device_id={"turn": peer},
            device_id_type=mesh_id,
        )

    keep = pltpu.make_async_copy(outbox.at[me], inbox.at[me], self_sem)

    def step(k):
        compress(extra + k)
        j = jnp.where(upward, k, blocks - 1 - k)
        start = pl.multiple_of(j * LANES, LANES)
        yr, yi = pick_rows(real, start, offsets), pick_rows(imag, start, offsets)
        re = (yr * cos - yi * sin).astype(BF16)
        im = (yr * sin + yi * cos).astype(BF16)
        for u in range(per):
            outbox[j * per + u, 0] = re[u * bin_local : (u + 1) * bin_local]
            outbox[j * per + u, 1] = im[u * bin_local : (u + 1) * bin_local]
        for v in range(per):
            peer = j * per + lax.rem(lane_of_me + v, per)

            @pl.when(peer != me)
            def _():
                message(peer, me).start()

        @pl.when(j == mine)
        def _():
            keep.start()

    if blocks <= 4:
        for k in range(blocks):
            step(k)
    else:
        pl.loop(0, blocks)(step)

    focus_maps(lambda r: rate[r], bin_local, turn_count, pulses, cos_map, sin_map)
    for load in loads[1:]:
        load.wait()
    keep.wait()

    def others(body):
        if turn_count <= 16:
            for off in range(1, turn_count):
                body(lax.rem(me + off, turn_count))
        else:
            pl.loop(1, turn_count)(lambda off: body(lax.rem(me + off, turn_count)))

    others(lambda peer: message(me, peer).wait_recv())
    azimuth(inbox, gm, gp, fm, fp, cos_map, sin_map, half, spec, out)
    others(lambda peer: message(peer, me).wait_send())


def local(raw_pulses, chirp_taps, knot_points, knot_index, spline_param, migration, azimuth_rate):
    turn_count = lax.axis_size("turn")
    pulses = raw_pulses.shape[1]
    taps_count = chirp_taps.shape[1]
    bin_local = azimuth_rate.shape[0]
    width = bin_local * turn_count + taps_count
    smem = pl.BlockSpec(memory_space=pltpu.SMEM)
    vmem = pl.BlockSpec(memory_space=pltpu.VMEM)
    hbm = pl.BlockSpec(memory_space=pl.ANY)
    gm = twiddle_np(turn_count, pulses, -1.0, 1.0)
    gp = twiddle_np(turn_count, pulses, 1.0, 1.0 / (turn_count * pulses))
    rows = turn_count * bin_local
    table = pltpu.VMEM((2 * pulses, 2 * pulses), BF16)
    turns = pltpu.VMEM((2, turn_count, pulses), F32)
    box = pltpu.VMEM((turn_count, 2, bin_local, pulses), BF16)
    return pl.pallas_call(
        kernel,
        in_specs=[smem] * 3 + [vmem] * 3 + [hbm] * 5,
        out_specs=vmem,
        out_shape=jax.ShapeDtypeStruct((2, bin_local, turn_count * pulses), F32),
        scratch_shapes=[
            pltpu.VMEM((2, pulses, width + MIGMAX), BF16),
            turns,
            turns,
            table,
            table,
            pltpu.VMEM((2 * LANES, taps_count + LANES), BF16),
            pltpu.VMEM((width - taps_count + MIGMAX, pulses), F32),
            pltpu.VMEM((width - taps_count + MIGMAX, pulses), F32),
            pltpu.VMEM((8, LANES), F32),
            pltpu.VMEM((8, LANES), F32),
            box,
            box,
            pltpu.VMEM((rows, pulses), F32),
            pltpu.VMEM((rows, pulses), F32),
            pltpu.VMEM((rows, 2 * pulses), BF16),
            pltpu.VMEM((rows, 2 * pulses), F32),
            pltpu.SemaphoreType.DMA((5,)),
            pltpu.SemaphoreType.DMA((2,)),
            pltpu.SemaphoreType.DMA((turn_count,)),
            pltpu.SemaphoreType.DMA((turn_count,)),
            pltpu.SemaphoreType.DMA,
        ],
        compiler_params=pltpu.CompilerParams(
            collective_id=0, has_side_effects=True, vmem_limit_bytes=60 * 2**20
        ),
    )(
        migration,
        knot_points,
        azimuth_rate,
        chirp_taps,
        knot_index.reshape(1, -1),
        spline_param.reshape(1, -1),
        raw_pulses,
        gm,
        gp,
        table_np(pulses, -1.0),
        table_np(pulses, 1.0),
    )


def solution(mesh):
    in_specs = (
        P(None, ("groups", "turn"), None),
        P(),
        P(("groups", "turn")),
        P(("groups", "turn")),
        P(("groups", "turn")),
        P(("groups", "turn")),
        P(("groups", "turn")),
    )
    out_specs = P(None, ("groups", "turn"), None)
    return jax.shard_map(local, mesh=mesh, in_specs=in_specs, out_specs=out_specs, check_vma=False)
```

```python
import functools
import math

import jax
import jax.numpy as jnp
import numpy as np
from jax import lax
from jax.experimental import pallas as pl
from jax.experimental.pallas import tpu as pltpu
from jax.sharding import PartitionSpec as P

BLK = 32
MIGMAX = 512
LANES = 128
F32 = jnp.float32
BF16 = jnp.bfloat16


def table_np(length, sign):
    line = np.arange(length)
    angles = (line[:, None] * line[None, :] % length) * (2.0 * math.pi / length)
    c, s = np.cos(angles), np.sin(angles) * sign
    return np.concatenate(
        [np.concatenate([c, s], 1), np.concatenate([-s, c], 1)], 0
    ).astype(BF16)


def twiddle_np(outer, inner, sign, scale):
    angles = (np.arange(outer)[:, None] * np.arange(inner)[None, :] % (outer * inner)) * (
        2.0 * math.pi / (outer * inner)
    )
    return np.stack([np.cos(angles) * scale, np.sin(angles) * sign * scale]).astype(np.float32)


def transform(values, sign):
    n = len(values)
    if n == 1:
        return values
    even = transform(values[0::2], sign)
    odd = transform(values[1::2], sign)
    low, high = [], []
    for k in range(n // 2):
        (er, ei), (zr, zi) = even[k], odd[k]
        if k == 0:
            tr, ti = zr, zi
        elif 4 * k == n:
            tr, ti = (-zi, zr) if sign > 0 else (zi, -zr)
        elif 8 * k == n:
            h = math.sqrt(0.5)
            tr, ti = ((zr - zi) * h, (zr + zi) * h) if sign > 0 else ((zr + zi) * h, (zi - zr) * h)
        elif 8 * k == 3 * n:
            h = math.sqrt(0.5)
            tr, ti = (
                ((-zr - zi) * h, (zr - zi) * h) if sign > 0 else ((zi - zr) * h, (-zr - zi) * h)
            )
        else:
            c = math.cos(2 * math.pi * k / n)
            s = math.sin(2 * math.pi * k / n) * sign
            tr, ti = zr * c - zi * s, zr * s + zi * c
        low.append((er + tr, ei + ti))
        high.append((er - tr, ei - ti))
    return low + high


def cos_sin_quarters(quarters):
    whole = jnp.floor(quarters + 0.5)
    x = (quarters - whole) * (0.5 * math.pi)
    n = whole.astype(jnp.int32)
    z = x * x
    s = x + x * z * ((-1.9515295891e-4 * z + 8.3321608736e-3) * z - 1.6666654611e-1)
    c = 1.0 - 0.5 * z + z * z * (
        (2.443315711809948e-5 * z - 1.388731625493765e-3) * z + 4.166664568298827e-2
    )
    odd = (n & 1) == 1
    cos = jnp.where(odd, s, c)
    sin = jnp.where(odd, c, s)
    cos = jnp.where(((n + 1) & 2) == 2, -cos, cos)
    sin = jnp.where((n & 2) == 2, -sin, sin)
    return cos, sin


def build_taps(chirp_ref, taps_ref, columns):
    sub = lax.broadcasted_iota(jnp.int32, (LANES, LANES), 0)
    lane = lax.broadcasted_iota(jnp.int32, (LANES, LANES), 1)
    keep = lane >= sub
    for d in range(2):
        before = jnp.zeros((LANES, LANES), F32)
        for block in range(columns + 1):
            if block < columns:
                row = chirp_ref[d : d + 1, block * LANES : (block + 1) * LANES].astype(F32)
                turned = pltpu.roll(
                    jnp.broadcast_to(row, (LANES, LANES)), 0, 1, stride=1, stride_axis=0
                )
            else:
                turned = jnp.zeros((LANES, LANES), F32)
            taps_ref[d * LANES : (d + 1) * LANES, block * LANES : (block + 1) * LANES] = jnp.where(
                keep, turned, before
            ).astype(BF16)
            before = turned


def pick_rows(ref, start, offsets):
    def chosen(x, bit):
        return (jnp.broadcast_to(offsets, x.shape) & bit) != 0

    bit = MIGMAX // 2
    size = LANES + bit
    low = ref[pl.ds(start, size), :]
    x = jnp.where(chosen(low, bit), ref[pl.ds(start + bit, size), :], low)
    while bit > 8:
        bit //= 2
        size = LANES + bit
        low = x[:size]
        x = jnp.where(chosen(low, bit), x[bit : bit + size], low)
    while bit > 1:
        bit //= 2
        x = jnp.where(chosen(x, bit), pltpu.roll(x, x.shape[0] - bit, 0), x)
    return x[:LANES]


def phases(knot_at, slots, knot_local, position):
    rest = 1.0 - position
    square = position * position
    cube = square * position
    weights = (
        rest * rest * rest / 6.0,
        (3.0 * cube - 6.0 * square + 4.0) / 6.0,
        (-3.0 * cube + 3.0 * square + 3.0 * position + 1.0) / 6.0,
        cube / 6.0,
    )
    displace = jnp.zeros_like(position)
    for step in range(4):
        value = jnp.zeros_like(position)
        for slot in range(slots):
            value = jnp.where(knot_local + step == slot, knot_at(slot), value)
        displace = displace + weights[step] * value
    return cos_sin_quarters(-8.0 * displace)


def compress_blocks(taps_ref, raw_ref, first, count, width, real_ref, imag_ref):
    starts = [(first + b) * LANES for b in range(count)]
    if not isinstance(first, int):
        starts = [pl.multiple_of(start, LANES) for start in starts]
    samples = jnp.concatenate(
        [raw_ref[c, :, pl.ds(start, width)] for start in starts for c in range(2)], axis=0
    )
    both = lax.dot_general(
        samples, taps_ref[...], (((1,), (1,)), ((), ())), preferred_element_type=F32
    )
    pulses = raw_ref.shape[1]
    for b, start in enumerate(starts):
        xr = both[2 * b * pulses : (2 * b + 1) * pulses]
        xi = both[(2 * b + 1) * pulses : (2 * b + 2) * pulses]
        real_ref[pl.ds(start, LANES), :] = (xr[:, :LANES] + xi[:, LANES:]).T
        imag_ref[pl.ds(start, LANES), :] = (xi[:, :LANES] - xr[:, LANES:]).T


def focus_maps(rate_at, bins, turn_count, inner, cos_ref, sin_ref):
    sub = lax.broadcasted_iota(jnp.int32, (bins, inner), 0)
    rate = jnp.zeros((bins, inner), F32)
    for r in range(bins):
        rate = jnp.where(sub == r, rate_at(r), rate)
    total = turn_count * inner
    lane = lax.broadcasted_iota(jnp.int32, (1, inner), 1)

    def one(k2):
        freq = k2 + turn_count * lane
        centred = jnp.where(freq < total // 2, freq, freq - total)
        quad = (centred * centred).astype(F32) * (2.0 / total)
        cos, sin = cos_sin_quarters(rate * quad)
        at = k2 * bins
        if not isinstance(k2, int):
            at = pl.multiple_of(at, bins)
        cos_ref[pl.ds(at, bins), :] = cos
        sin_ref[pl.ds(at, bins), :] = sin

    if turn_count <= 16:
        for k2 in range(turn_count):
            one(k2)
    else:
        pl.loop(0, turn_count)(one)


def azimuth(inbox_ref, gm_ref, gp_ref, fm_ref, fp_ref, cos_ref, sin_ref, half_ref, spec_ref, out_ref):
    turn_count, _, bins, inner = inbox_ref.shape
    step = 16
    rows = turn_count * bins
    chunk = min(rows, 512)
    for r in range(0, bins, step):
        values = [
            (
                inbox_ref[s, 0, r : r + step, :].astype(F32),
                inbox_ref[s, 1, r : r + step, :].astype(F32),
            )
            for s in range(turn_count)
        ]
        for k2, (re, im) in enumerate(transform(values, -1)):
            if k2:
                gr, gi = gm_ref[0, k2 : k2 + 1, :], gm_ref[1, k2 : k2 + 1, :]
                re, im = re * gr - im * gi, re * gi + im * gr
            at = k2 * bins + r
            half_ref[at : at + step, :inner] = re.astype(BF16)
            half_ref[at : at + step, inner:] = im.astype(BF16)
    for at in range(0, rows, chunk):
        here = slice(at, at + chunk)
        spec = jnp.dot(half_ref[here, :], fm_ref[...], preferred_element_type=F32)
        sr, si = spec[:, :inner], spec[:, inner:]
        cr, ci = cos_ref[here, :], sin_ref[here, :]
        half_ref[here, :inner] = (sr * cr - si * ci).astype(BF16)
        half_ref[here, inner:] = (sr * ci + si * cr).astype(BF16)
    for at in range(0, rows, chunk):
        here = slice(at, at + chunk)
        spec_ref[here, :] = jnp.dot(half_ref[here, :], fp_ref[...], preferred_element_type=F32)
    for r in range(0, bins, step):
        values = []
        for k2 in range(turn_count):
            at = k2 * bins + r
            re, im = spec_ref[at : at + step, :inner], spec_ref[at : at + step, inner:]
            gr, gi = gp_ref[0, k2 : k2 + 1, :], gp_ref[1, k2 : k2 + 1, :]
            values.append((re * gr - im * gi, re * gi + im * gr))
        for n2, (re, im) in enumerate(transform(values, 1)):
            out_ref[0, r : r + step, n2 * inner : (n2 + 1) * inner] = re
            out_ref[1, r : r + step, n2 * inner : (n2 + 1) * inner] = im


def kernel(
    migration, knots, rate, chirp, index, position, raw_hbm, gm_hbm, gp_hbm, fm_hbm, fp_hbm,
    out,
    raw, gm, gp, fm, fp, taps, real, imag, own_knots, next_knots, outbox, inbox, cos_map, sin_map, half, spec,
    load_sem, knot_sem, send_sem, recv_sem, self_sem,
):
    turn_count, _, bin_local, pulses = inbox.shape
    knot_count = knots.shape[0]
    per = LANES // bin_local
    blocks = turn_count // per
    columns = chirp.shape[1] // LANES
    me = lax.axis_index("turn")
    mine, lane_of_me = lax.div(me, per), lax.rem(me, per)
    mesh_id = pl.DeviceIdType.MESH
    loads = [
        pltpu.make_async_copy(src, dst, load_sem.at[i])
        for i, (src, dst) in enumerate(
            [
                (raw_hbm.at[:, :, pl.ds(0, raw.shape[2])], raw),
                (gm_hbm, gm),
                (gp_hbm, gp),
                (fm_hbm, fm),
                (fp_hbm, fp),
            ]
        )
    ]
    for load in loads:
        load.start()
    barrier = pltpu.get_barrier_semaphore()

    def greet(off):
        pl.semaphore_signal(
            barrier, inc=1, device_id={"turn": lax.rem(me + off, turn_count)}, device_id_type=mesh_id
        )

    if turn_count <= 16:
        for off in range(1, turn_count):
            greet(off)
    else:
        pl.loop(1, turn_count)(greet)
    for j in range(min(knot_count, 8)):
        own_knots[j : j + 1, :] = jnp.full((1, LANES), knots[j], F32)
    build_taps(chirp, taps, columns)
    width = (columns + 1) * LANES
    extra = MIGMAX // LANES
    loads[0].wait()
    group = 8 if (blocks + extra) % 8 == 0 else 4

    def compress(i):
        compress_blocks(taps, raw, i * group, group, width, real, imag)

    if blocks + extra == group:
        compress(0)
    else:
        pl.loop(0, (blocks + extra) // group)(compress)
    pulse = lax.broadcasted_iota(jnp.int32, (1, pulses), 1)
    offsets = jnp.zeros((1, pulses), jnp.int32)
    for block in range(pulses // BLK):
        offsets = jnp.where(pulse // BLK == block, migration[block], offsets)

    def pick(j):
        start = j * LANES
        if not isinstance(j, int):
            start = pl.multiple_of(start, LANES)
        real[pl.ds(start, LANES), :] = pick_rows(real, start, offsets)
        imag[pl.ds(start, LANES), :] = pick_rows(imag, start, offsets)

    if blocks <= 4:
        for j in range(blocks):
            pick(j)
    else:
        pl.loop(0, blocks)(pick)
    pl.semaphore_wait(barrier, turn_count - 1)
    knot_copy = pltpu.make_async_remote_copy(
        src_ref=own_knots,
        dst_ref=next_knots,
        send_sem=knot_sem.at[0],
        recv_sem=knot_sem.at[1],
        device_id={"turn": lax.rem(me + turn_count - 1, turn_count)},
        device_id_type=mesh_id,
    )
    knot_copy.start()
    upward = mine >= blocks // 2
    knot_copy.wait()
    past = jnp.where(me == turn_count - 1, 0.0, 1.0).astype(F32)

    def knot_at(slot):
        if slot < knot_count:
            return knots[slot]
        return next_knots[slot - knot_count : slot - knot_count + 1, :] * past

    cos, sin = phases(knot_at, knot_count + 3, index[...] - me * knot_count, position[...])
    def message(peer, sender):
        return pltpu.make_async_remote_copy(
            src_ref=outbox.at[peer],
            dst_ref=inbox.at[sender],
            send_sem=send_sem.at[peer],
            recv_sem=recv_sem.at[sender],
            device_id={"turn": peer},
            device_id_type=mesh_id,
        )

    keep = pltpu.make_async_copy(outbox.at[me], inbox.at[me], self_sem)

    def step(k):
        j = jnp.where(upward, k, blocks - 1 - k)
        start = pl.multiple_of(j * LANES, LANES)
        yr, yi = real[pl.ds(start, LANES), :], imag[pl.ds(start, LANES), :]
        re = (yr * cos - yi * sin).astype(BF16)
        im = (yr * sin + yi * cos).astype(BF16)
        for u in range(per):
            outbox[j * per + u, 0] = re[u * bin_local : (u + 1) * bin_local]
            outbox[j * per + u, 1] = im[u * bin_local : (u + 1) * bin_local]
        for v in range(per):
            peer = j * per + lax.rem(lane_of_me + v, per)

            @pl.when(peer != me)
            def _():
                message(peer, me).start()

        @pl.when(j == mine)
        def _():
            keep.start()

    if blocks <= 4:
        for k in range(blocks):
            step(k)
    else:
        pl.loop(0, blocks)(step)

    focus_maps(lambda r: rate[r], bin_local, turn_count, pulses, cos_map, sin_map)
    for load in loads[1:]:
        load.wait()
    keep.wait()

    def others(body):
        if turn_count <= 16:
            for off in range(1, turn_count):
                body(lax.rem(me + off, turn_count))
        else:
            pl.loop(1, turn_count)(lambda off: body(lax.rem(me + off, turn_count)))

    others(lambda peer: message(me, peer).wait_recv())
    azimuth(inbox, gm, gp, fm, fp, cos_map, sin_map, half, spec, out)
    others(lambda peer: message(peer, me).wait_send())


def local(raw_pulses, chirp_taps, knot_points, knot_index, spline_param, migration, azimuth_rate):
    turn_count = lax.axis_size("turn")
    pulses = raw_pulses.shape[1]
    taps_count = chirp_taps.shape[1]
    bin_local = azimuth_rate.shape[0]
    width = bin_local * turn_count + taps_count
    smem = pl.BlockSpec(memory_space=pltpu.SMEM)
    vmem = pl.BlockSpec(memory_space=pltpu.VMEM)
    hbm = pl.BlockSpec(memory_space=pl.ANY)
    gm = twiddle_np(turn_count, pulses, -1.0, 1.0)
    gp = twiddle_np(turn_count, pulses, 1.0, 1.0 / (turn_count * pulses))
    rows = turn_count * bin_local
    table = pltpu.VMEM((2 * pulses, 2 * pulses), BF16)
    turns = pltpu.VMEM((2, turn_count, pulses), F32)
    box = pltpu.VMEM((turn_count, 2, bin_local, pulses), BF16)
    return pl.pallas_call(
        kernel,
        in_specs=[smem] * 3 + [vmem] * 3 + [hbm] * 5,
        out_specs=vmem,
        out_shape=jax.ShapeDtypeStruct((2, bin_local, turn_count * pulses), F32),
        scratch_shapes=[
            pltpu.VMEM((2, pulses, width + MIGMAX), BF16),
            turns,
            turns,
            table,
            table,
            pltpu.VMEM((2 * LANES, taps_count + LANES), BF16),
            pltpu.VMEM((width - taps_count + MIGMAX, pulses), F32),
            pltpu.VMEM((width - taps_count + MIGMAX, pulses), F32),
            pltpu.VMEM((8, LANES), F32),
            pltpu.VMEM((8, LANES), F32),
            box,
            box,
            pltpu.VMEM((rows, pulses), F32),
            pltpu.VMEM((rows, pulses), F32),
            pltpu.VMEM((rows, 2 * pulses), BF16),
            pltpu.VMEM((rows, 2 * pulses), F32),
            pltpu.SemaphoreType.DMA((5,)),
            pltpu.SemaphoreType.DMA((2,)),
            pltpu.SemaphoreType.DMA((turn_count,)),
            pltpu.SemaphoreType.DMA((turn_count,)),
            pltpu.SemaphoreType.DMA,
        ],
        compiler_params=pltpu.CompilerParams(
            collective_id=0, has_side_effects=True, vmem_limit_bytes=60 * 2**20
        ),
    )(
        migration,
        knot_points,
        azimuth_rate,
        chirp_taps,
        knot_index.reshape(1, -1),
        spline_param.reshape(1, -1),
        raw_pulses,
        gm,
        gp,
        table_np(pulses, -1.0),
        table_np(pulses, 1.0),
    )


def solution(mesh):
    in_specs = (
        P(None, ("groups", "turn"), None),
        P(),
        P(("groups", "turn")),
        P(("groups", "turn")),
        P(("groups", "turn")),
        P(("groups", "turn")),
        P(("groups", "turn")),
    )
    out_specs = P(None, ("groups", "turn"), None)
    return jax.shard_map(local, mesh=mesh, in_specs=in_specs, out_specs=out_specs, check_vma=False)
```
